32 devices in a mesh: parts: 2 (over y), tm: 4 (over z), chan: 4 (over x, core).
Axes of the slice: x: 2, y: 2, z: 4, core: 2. Of those that a mesh axis runs over, the one named last changes fastest.
Arguments:
- records: float32 [512, 1024], P(('parts', 'chan'), 'tm'), parts along dimension 0, may hold values from -8 to 8
- fir_taps: float32 [129], replicated, may hold values from -0.5 to 0.5
- matchings: int32 [2, 4], replicated, may hold values from 0 to 3, as said below
Outputs:
- correlograms: bfloat16 [2, 8, 64, 16448], P(None, ('parts', 'chan'), 'tm'), parts along dimension 1
The draws below stay inside these ranges and needn't reach their ends.
There are 2 independent parts, one for each index of `parts`. The reference program is written for one: setup_inputs(seed, part) draws one part's arguments, and reference() takes and returns one part's arrays. A program takes and returns all parts, laid end to end along the dimension named above; an argument that names none is the same for every part. Nothing has to cross between parts.
Inputs may be any that keep to these rules, and one draw needn't show every extreme that they name: `matchings`: each row sends every group to another group, and following a row from any group visits all 4 groups in one cycle.
All inputs are finite; a program needn't handle non-finite values.
Results may differ from the reference program's by a relative error of at most 0.0049.
Values may be sent and summed in bfloat16 or wider, within the bound.
A program may use at most 64 MiB of HBM per device.

```python
import math
import jax
import jax.numpy as jnp
from jax import lax

GROUP_CH = 64
TAPS = 129
AVG = 65
MAXLAG = 128
MATCH = 2
LAGS = 257
GROUPS = 4
CHANNELS = 256
SAMPLES = 1024


def draw_matchings(key, part):
    tables_list = []
    for match_index in range(MATCH):
        visiting = jax.random.permutation(jax.random.fold_in(key, 17 + match_index), GROUPS)
        following = jnp.roll(visiting, -1)
        successor = jnp.zeros((GROUPS,), jnp.int32).at[visiting].set(following.astype(jnp.int32))
        tables_list.append(successor)
    return jnp.stack(tables_list).astype(jnp.int32)


def block_levels(key, extent, shards, low, high):
    factor_of, own = 1.0, jax.random.fold_in(key, 6)
    for dim, shards_of in shards:
        heights = jnp.exp(jax.random.uniform(jax.random.fold_in(own, dim), (shards_of,), jnp.float32, low / len(shards), high / len(shards)))
        factor_of = factor_of * jnp.repeat(heights, extent[dim] // shards_of).reshape([-1 if axis == dim else 1 for axis in range(len(extent))])
    return factor_of


def bell_draw(rng, shape, width, bound, split=(), kind=jnp.bfloat16):
    drawn = width * jax.random.normal(rng, shape, jnp.float32)
    if split:
        drawn = drawn * block_levels(rng, shape, split, -0.22, 0.18)
    return jnp.clip(drawn, -bound, bound).astype(kind)


def setup_inputs(seed: int = 0, part: int = 0) -> dict:
    keys = jax.random.split(jax.random.key(seed), 4)
    own_keys = jax.random.split(jax.random.fold_in(keys[3], part), 4)
    return {
        "records": bell_draw(own_keys[0], (CHANNELS, SAMPLES), 1.0, 8.0, ((0, 4), (1, 4)), jnp.float32),
        "fir_taps": bell_draw(keys[1], (TAPS,), TAPS ** -0.5, 0.5, (), jnp.float32),
        "matchings": draw_matchings(jax.random.fold_in(keys[3], 71), part),
    }


EPSILON = 1e-05

def preprocess(records, fir_taps):
    samples = records.shape[1]
    half_taps = fir_taps.shape[0] // 2
    padded = jnp.pad(records, ((0, 0), (half_taps, half_taps)))
    filtered = jnp.zeros_like(records)
    for tap_index in range(fir_taps.shape[0]):
        begin_at = 2 * half_taps - tap_index
        filtered = filtered + fir_taps[tap_index] * padded[:, begin_at:begin_at + samples]
    half_avg = AVG // 2
    magnitude = jnp.pad(jnp.abs(filtered), ((0, 0), (half_avg, half_avg)))
    window_sum = jnp.zeros_like(records)
    for shift_index in range(AVG):
        window_sum = window_sum + magnitude[:, shift_index:shift_index + samples]
    local_mean = window_sum / AVG
    return (filtered / (local_mean + EPSILON)).astype(jnp.bfloat16)

def correlate_group(own_rows, partner_rows):
    samples = own_rows.shape[1]
    length = samples + 2 * MAXLAG
    own_spec = jnp.fft.rfft(own_rows.astype(jnp.float32), n=length, axis=1)
    partner_spec = jnp.fft.rfft(partner_rows.astype(jnp.float32), n=length, axis=1)
    cross = jnp.conj(own_spec)[:, None, :] * partner_spec[None, :, :]
    circular = jnp.fft.irfft(cross, n=length, axis=2)
    lagged = jnp.concatenate([circular[:, :, length - MAXLAG:], circular[:, :, :MAXLAG + 1]], axis=2)
    return jnp.transpose(lagged, (0, 2, 1))

def reference(records, fir_taps, matchings):
    normed = preprocess(records, fir_taps)
    samples = records.shape[1]
    grouped = normed.reshape(GROUPS, GROUP_CH, samples)
    scaling = 1.0 / math.sqrt(samples)
    results = []
    for match_index in range(MATCH):
        partners = grouped[matchings[match_index]]
        per_group = lax.map(lambda paired: correlate_group(paired[0], paired[1]), (grouped, partners))
        shaped = (per_group * scaling).reshape(GROUPS, GROUP_CH, LAGS * GROUP_CH)
        results.append(shaped.astype(jnp.bfloat16))
    return jnp.stack(results)
```

```python
import functools
import math

import jax
import jax.numpy as jnp
from jax import lax
from jax.experimental import pallas as pl
from jax.experimental.pallas import tpu as pltpu
from jax.sharding import PartitionSpec as P

AVG = 65
MAXLAG = 128
LAGS = 257


EPSILON = 1e-05


def extended_2(cells, sides, width):
    for axis, dim in sides:
        count = lax.axis_size(axis)
        ends = count - 1
        head = lax.slice_in_dim(cells, 0, width, axis=dim)
        tail = lax.slice_in_dim(cells, cells.shape[dim] - width, cells.shape[dim], axis=dim)
        cells = jnp.concatenate(
            [
                lax.ppermute(tail, axis, [(i, (i + 1) % count) for i in range(ends)]),
                cells,
                lax.ppermute(head, axis, [((i + 1) % count, i) for i in range(ends)]),
            ],
            axis=dim,
        )
    return cells


def falling(window, row_count):
    leading = window.shape[:-1]
    extended = jnp.concatenate([window, jnp.zeros(leading + (1,), window.dtype)], axis=-1)
    span_width = extended.shape[-1]
    repeated = jnp.broadcast_to(extended[..., None, :], leading + (row_count, span_width))
    repeated = repeated.reshape(leading + (row_count * span_width,))[
        ..., : row_count * (span_width - 1)
    ]
    return repeated.reshape(leading + (row_count, span_width - 1))[..., row_count - 1 :]


def fir_matrix(fir_taps, row_count, col_count):
    tap_count = fir_taps.shape[0]
    padded = jnp.concatenate(
        [
            jnp.zeros((row_count - tap_count,), jnp.float32),
            fir_taps,
            jnp.zeros((col_count - 1,), jnp.float32),
        ]
    )
    return falling(padded, row_count)


def normalize(records, fir_taps):
    tap_half = fir_taps.shape[0] // 2
    avg_half = AVG // 2
    samples_dev = records.shape[1]
    widened = extended_2(records, (("tm", 1),), tap_half + avg_half)
    filtered = jnp.dot(
        widened,
        fir_matrix(fir_taps, samples_dev + 2 * (tap_half + avg_half), samples_dev + 2 * avg_half),
        precision=lax.Precision.HIGHEST,
        preferred_element_type=jnp.float32,
    )
    global_time = (
        lax.axis_index("tm") * samples_dev
        - avg_half
        + lax.iota(jnp.int32, samples_dev + 2 * avg_half)
    )
    inside = (global_time >= 0) & (global_time < samples_dev * lax.axis_size("tm"))
    filtered = jnp.where(inside[None, :], filtered, 0.0)
    magnitude = jnp.abs(filtered)
    rows_at = lax.broadcasted_iota(jnp.int32, (samples_dev + 2 * avg_half, samples_dev), 0)
    cols_at = lax.broadcasted_iota(jnp.int32, (samples_dev + 2 * avg_half, samples_dev), 1)
    band_matrix = ((rows_at >= cols_at) & (rows_at <= cols_at + 2 * avg_half)).astype(jnp.float32)
    local_mean = (
        jnp.dot(
            magnitude,
            band_matrix,
            precision=lax.Precision.HIGHEST,
            preferred_element_type=jnp.float32,
        )
        / AVG
    )
    centre = filtered[:, avg_half : avg_half + samples_dev]
    return (centre / (local_mean + EPSILON)).astype(jnp.bfloat16)


def correlate(row_share, scaling, own_ref, partners_ref, out_ref):
    rows, samples = own_ref.shape
    match_count, group_ch, _ = partners_ref.shape
    depth = samples + MAXLAG
    width = samples + 2 * MAXLAG
    margin = jnp.zeros((rows, MAXLAG), jnp.bfloat16)
    own = jnp.concatenate([margin, own_ref[...], margin], axis=1).astype(jnp.float32)
    tail = jnp.zeros((group_ch, MAXLAG), jnp.bfloat16)
    weights = []
    for match in range(match_count):
        ahead = jnp.concatenate([partners_ref[match], tail], axis=1)
        behind = pltpu.roll(ahead.astype(jnp.float32), 1, 1).astype(jnp.bfloat16)
        weights += [behind, ahead]
    weights = jnp.concatenate(weights, axis=0)
    pair = 2 * group_ch
    per_chunk = 16
    for first in range(0, LAGS, 2 * per_chunk):
        lags = range(first, min(first + 2 * per_chunk, LAGS), 2)
        lagged = jnp.concatenate(
            [
                pltpu.roll(own, (lag - (2 * MAXLAG - 1)) % width, 1)[:, :depth].astype(jnp.bfloat16)
                for lag in lags
            ],
            axis=0,
        )
        summed = lax.dot_general(
            lagged, weights, (((1,), (1,)), ((), ())), preferred_element_type=jnp.float32
        )
        scaled = (summed * scaling).astype(jnp.bfloat16)
        for at, lag in enumerate(lags):
            span = min(pair, (LAGS - lag) * group_ch)
            for match in range(match_count):
                out_ref[match, 0, :, lag * group_ch : lag * group_ch + span] = scaled[
                    at * rows : at * rows + row_share, match * pair : match * pair + span
                ]


def local(records, fir_taps, matchings):
    normed = normalize(records, fir_taps)
    group_ch, samples_dev = normed.shape
    group_count = lax.axis_size("chan")
    group_index = lax.axis_index("chan")
    match_count = matchings.shape[0]
    every_group = lax.all_gather(normed, "chan", axis=0, tiled=True).reshape(
        group_count, group_ch, samples_dev
    )
    partners = jnp.take(every_group, matchings[:, group_index], axis=0)
    time_count = lax.axis_size("tm")
    scaling = 1.0 / math.sqrt(samples_dev * time_count)
    row_share = group_ch // time_count
    own_rows = lax.all_to_all(normed, "tm", split_axis=0, concat_axis=1, tiled=True)
    incoming = lax.all_gather(partners, "tm", axis=2, tiled=True)
    rows = -(-row_share // 16) * 16
    own_rows = jnp.pad(own_rows, ((0, rows - row_share), (0, 0)))
    return pl.pallas_call(
        functools.partial(correlate, row_share, scaling),
        out_shape=jax.ShapeDtypeStruct(
            (match_count, 1, row_share, LAGS * group_ch), jnp.bfloat16
        ),
        in_specs=[pl.BlockSpec(memory_space=pltpu.VMEM)] * 2,
        out_specs=pl.BlockSpec(memory_space=pltpu.VMEM),
    )(own_rows, incoming)


def solution(mesh):
    in_specs = (P(("parts", "chan"), "tm"), P(), P())
    out_specs = P(None, ("parts", "chan"), "tm", None)
    return jax.shard_map(local, mesh=mesh, in_specs=in_specs, out_specs=out_specs, check_vma=False)
```

```python
import functools
import math

import jax
import jax.numpy as jnp
from jax import lax
from jax.experimental import pallas as pl
from jax.experimental.pallas import tpu as pltpu
from jax.sharding import PartitionSpec as P

AVG = 65
MAXLAG = 128
LAGS = 257
HALO = 128
CORES = 2

EPSILON = 1e-05


def split(values):
    high = values.astype(jnp.bfloat16)
    low = (values - high.astype(jnp.float32)).astype(jnp.bfloat16)
    return high, low


def flipped(at, step, count):
    if count & (count - 1):
        return lax.rem(at + step, count)
    bit = 1
    while bit <= step:
        if step & bit:
            at = at + bit * (1 - 2 * lax.rem(at // bit, 2))
        bit *= 2
    return at


def gather(
    time_count,
    group_count,
    records_ref,
    taps_ref,
    every_ref,
    wide,
    taps_row,
    halo_send,
    halo_recv,
    send_sem,
    recv_sem,
):
    time_at, chan_at = lax.axis_index("tm"), lax.axis_index("chan")
    channels, samples = records_ref.shape
    width = samples + 2 * HALO
    chips = group_count // CORES
    chip_at, core_at = chan_at // CORES, lax.rem(chan_at, CORES)
    sibling = {"chan": chan_at + 1 - 2 * core_at}
    times = [flipped(time_at, step, time_count) for step in range(time_count)]
    others = [
        lax.rem(chip_at + step, chips) * CORES + core_at for step in range(1, chips)
    ]

    barrier = pltpu.get_barrier_semaphore()
    peers = [{"tm": at} for at in times[1:]] + [{"chan": at} for at in others] + [sibling]
    for peer in peers:
        pl.semaphore_signal(barrier, inc=1, device_id=peer)

    taps_row[...] = jnp.zeros_like(taps_row)
    taps_row[0:1, 0 : taps_ref.shape[1]] = taps_ref[...]
    tap_half = taps_ref.shape[1] // 2
    fir = pltpu.roll(
        jnp.broadcast_to(taps_row[0:1, :], (width, width)),
        width - tap_half,
        1,
        stride=1,
        stride_axis=0,
    )
    fir_high, fir_low = split(fir)
    pl.semaphore_wait(barrier, len(peers))

    def halo(source, target, side, to):
        return pltpu.make_async_remote_copy(
            src_ref=records_ref.at[:, source],
            dst_ref=wide.at[:, target],
            send_sem=halo_send.at[side],
            recv_sem=halo_recv.at[side],
            device_id={"tm": to},
        )

    to_next = halo(pl.ds(samples - HALO, HALO), pl.ds(0, HALO), 0, time_at + 1)
    to_last = halo(pl.ds(0, HALO), pl.ds(samples + HALO, HALO), 1, time_at - 1)
    has_next, has_last = time_at < time_count - 1, time_at > 0
    pl.when(has_next)(to_next.start)
    pl.when(has_last)(to_last.start)
    wide[:, HALO : HALO + samples] = records_ref[...]

    @pl.when(jnp.logical_not(has_last))
    def _():
        wide[:, 0:HALO] = jnp.zeros((channels, HALO), jnp.float32)

    @pl.when(jnp.logical_not(has_next))
    def _():
        wide[:, samples + HALO : width] = jnp.zeros((channels, HALO), jnp.float32)

    pl.when(has_last)(to_next.wait_recv)
    pl.when(has_next)(to_last.wait_recv)

    high, low = split(wide[...])
    both = jnp.dot(
        jnp.concatenate([high, low], axis=0), fir_high, preferred_element_type=jnp.float32
    )
    filtered = (
        both[0:channels]
        + both[channels : 2 * channels]
        + jnp.dot(high, fir_low, preferred_element_type=jnp.float32)
    )
    at = time_at * samples - HALO + lax.broadcasted_iota(jnp.int32, (channels, width), 1)
    filtered = jnp.where((at >= 0) & (at < samples * time_count), filtered, 0.0)
    rows_at = lax.broadcasted_iota(jnp.int32, (width, samples), 0)
    cols_at = lax.broadcasted_iota(jnp.int32, (width, samples), 1) + HALO
    band = (jnp.abs(rows_at - cols_at) <= AVG // 2).astype(jnp.float32).astype(jnp.bfloat16)
    summed = jnp.dot(
        jnp.concatenate(split(jnp.abs(filtered)), axis=0), band, preferred_element_type=jnp.float32
    )
    local_mean = (summed[0:channels] + summed[channels : 2 * channels]) / AVG
    centre = filtered[:, HALO : HALO + samples]
    every_ref[chan_at, time_at] = (centre / (local_mean + EPSILON)).astype(jnp.bfloat16)

    sent = []

    def push(chan_from, time_from, to):
        block = every_ref.at[chan_from, time_from]
        copy = pltpu.make_async_remote_copy(
            src_ref=block,
            dst_ref=block,
            send_sem=send_sem.at[len(sent)],
            recv_sem=recv_sem.at[chan_from, time_from],
            device_id=to,
        )
        copy.start()
        sent.append(copy)

    def arrived(chan_from, time_from):
        block = every_ref.at[chan_from, time_from]
        pltpu.make_async_remote_copy(
            src_ref=block,
            dst_ref=block,
            send_sem=send_sem.at[0],
            recv_sem=recv_sem.at[chan_from, time_from],
            device_id=sibling,
        ).wait_recv()

    for time_to in reversed(times[1:]):
        push(chan_at, time_at, {"tm": time_to})
    for step, time_from in enumerate(times):
        if step:
            arrived(chan_at, time_from)
        for chan_to in others:
            push(chan_at, time_from, {"chan": chan_to})
        push(chan_at, time_from, sibling)
        if step:
            for chan_from in others:
                arrived(chan_from, times[step - 1])
                push(chan_from, times[step - 1], sibling)
    for chan_from in others:
        arrived(chan_from, times[-1])
        push(chan_from, times[-1], sibling)
    for time_from in times:
        for chan_from in [chan_at] + others:
            arrived(chan_from + 1 - 2 * core_at, time_from)
    for copy in sent:
        copy.wait_send()
    pl.when(has_next)(to_next.wait_send)
    pl.when(has_last)(to_last.wait_send)


def correlate(row_share, scaling, matchings_ref, every_ref, out_ref):
    _, time_count, group_ch, samples_dev = every_ref.shape
    match_count = matchings_ref.shape[0]
    samples = time_count * samples_dev
    chan_at, time_at = lax.axis_index("chan"), lax.axis_index("tm")
    depth = samples + MAXLAG
    width = samples + 2 * MAXLAG
    rows = -(-row_share // 16) * 16
    row_at = time_at * row_share
    start = pl.multiple_of(row_at // rows * rows, rows)
    margin = jnp.zeros((rows, MAXLAG), jnp.bfloat16)
    blocks = [every_ref[chan_at, at, pl.ds(start, rows), :] for at in range(time_count)]
    own = jnp.concatenate([margin] + blocks + [margin], axis=1).astype(jnp.float32)
    if rows != row_share:
        own = pltpu.roll(own, rows - lax.rem(row_at, rows), 0)
    tail = jnp.zeros((group_ch, MAXLAG), jnp.bfloat16)
    weights = []
    for match in range(match_count):
        partner = matchings_ref[match, chan_at]
        blocks = [every_ref[partner, at] for at in range(time_count)]
        ahead = jnp.concatenate(blocks + [tail], axis=1)
        behind = pltpu.roll(ahead.astype(jnp.float32), 1, 1).astype(jnp.bfloat16)
        weights += [behind, ahead]
    weights = jnp.concatenate(weights, axis=0)
    pair = 2 * group_ch
    per_chunk = 16
    for first in range(0, LAGS, 2 * per_chunk):
        lags = range(first, min(first + 2 * per_chunk, LAGS), 2)
        lagged = jnp.concatenate(
            [
                pltpu.roll(own, (lag - (2 * MAXLAG - 1)) % width, 1)[:, :depth].astype(jnp.bfloat16)
                for lag in lags
            ],
            axis=0,
        )
        summed = lax.dot_general(
            lagged, weights, (((1,), (1,)), ((), ())), preferred_element_type=jnp.float32
        )
        scaled = (summed * scaling).astype(jnp.bfloat16)
        for at, lag in enumerate(lags):
            span = min(pair, (LAGS - lag) * group_ch)
            for match in range(match_count):
                out_ref[match, 0, :, lag * group_ch : lag * group_ch + span] = scaled[
                    at * rows : at * rows + row_share, match * pair : match * pair + span
                ]


def local(records, fir_taps, matchings):
    group_ch, samples_dev = records.shape
    group_count, time_count = lax.axis_size("chan"), lax.axis_size("tm")
    match_count = matchings.shape[0]
    width = samples_dev + 2 * HALO
    chips = group_count // CORES
    sends = time_count - 1 + time_count * (2 * chips - 1)
    every = pl.pallas_call(
        functools.partial(gather, time_count, group_count),
        out_shape=jax.ShapeDtypeStruct(
            (group_count, time_count, group_ch, samples_dev), jnp.bfloat16
        ),
        in_specs=[pl.BlockSpec(memory_space=pltpu.VMEM)] * 2,
        out_specs=pl.BlockSpec(memory_space=pltpu.VMEM),
        scratch_shapes=[
            pltpu.VMEM((group_ch, width), jnp.float32),
            pltpu.VMEM((8, width), jnp.float32),
            pltpu.SemaphoreType.DMA((2,)),
            pltpu.SemaphoreType.DMA((2,)),
            pltpu.SemaphoreType.DMA((sends,)),
            pltpu.SemaphoreType.DMA((group_count, time_count)),
        ],
        compiler_params=pltpu.CompilerParams(collective_id=0, has_side_effects=True),
    )(records, fir_taps.reshape(1, -1))
    row_share = group_ch // time_count
    scaling = 1.0 / math.sqrt(samples_dev * time_count)
    return pl.pallas_call(
        functools.partial(correlate, row_share, scaling),
        out_shape=jax.ShapeDtypeStruct(
            (match_count, 1, row_share, LAGS * group_ch), jnp.bfloat16
        ),
        in_specs=[
            pl.BlockSpec(memory_space=pltpu.SMEM),
            pl.BlockSpec(memory_space=pltpu.VMEM),
        ],
        out_specs=pl.BlockSpec(memory_space=pltpu.VMEM),
    )(matchings, every)


def solution(mesh):
    in_specs = (P(("parts", "chan"), "tm"), P(), P())
    out_specs = P(None, ("parts", "chan"), "tm", None)
    return jax.shard_map(local, mesh=mesh, in_specs=in_specs, out_specs=out_specs, check_vma=False)
```

```python
import functools
import math

import jax
import jax.numpy as jnp
from jax import lax
from jax.experimental import pallas as pl
from jax.experimental.pallas import tpu as pltpu
from jax.sharding import PartitionSpec as P

AVG = 65
MAXLAG = 128
LAGS = 257
HALO = 128
CORES = 2

EPSILON = 1e-05


def split(values):
    high = values.astype(jnp.bfloat16)
    low = (values - high.astype(jnp.float32)).astype(jnp.bfloat16)
    return high, low


def gather(
    time_count,
    group_count,
    records_ref,
    taps_ref,
    every_ref,
    wide,
    taps_row,
    halo_send,
    halo_recv,
    send_sem,
    recv_sem,
):
    time_at, chan_at = lax.axis_index("tm"), lax.axis_index("chan")
    channels, samples = records_ref.shape
    width = samples + 2 * HALO
    chips = group_count // CORES
    chip_at, core_at = chan_at // CORES, lax.rem(chan_at, CORES)
    sibling = {"chan": chan_at + 1 - 2 * core_at}
    times = [time_at] + [
        step + (step >= time_at).astype(jnp.int32) for step in range(time_count - 1)
    ]
    has_next, has_last = time_at < time_count - 1, time_at > 0
    others = [
        lax.rem(chip_at + step, chips) * CORES + core_at for step in range(1, chips)
    ]

    barrier = pltpu.get_barrier_semaphore()
    peers = [{"chan": at} for at in others] + [sibling]
    for present, at in ((has_next, time_at + 1), (has_last, time_at - 1)):
        pl.when(present)(
            functools.partial(pl.semaphore_signal, barrier, inc=1, device_id={"tm": at})
        )
    for peer in peers:
        pl.semaphore_signal(barrier, inc=1, device_id=peer)

    taps_row[...] = jnp.zeros_like(taps_row)
    taps_row[0:1, 0 : taps_ref.shape[1]] = taps_ref[...]
    tap_half = taps_ref.shape[1] // 2
    fir = pltpu.roll(
        jnp.broadcast_to(taps_row[0:1, :], (width, width)),
        width - tap_half,
        1,
        stride=1,
        stride_axis=0,
    )
    fir_high, fir_low = split(fir)
    pl.semaphore_wait(
        barrier, len(peers) + has_next.astype(jnp.int32) + has_last.astype(jnp.int32)
    )

    def halo(source, target, side, to):
        return pltpu.make_async_remote_copy(
            src_ref=records_ref.at[:, source],
            dst_ref=wide.at[:, target],
            send_sem=halo_send.at[side],
            recv_sem=halo_recv.at[side],
            device_id={"tm": to},
        )

    to_next = halo(pl.ds(samples - HALO, HALO), pl.ds(0, HALO), 0, time_at + 1)
    to_last = halo(pl.ds(0, HALO), pl.ds(samples + HALO, HALO), 1, time_at - 1)
    pl.when(has_next)(to_next.start)
    pl.when(has_last)(to_last.start)
    wide[:, HALO : HALO + samples] = records_ref[...]

    @pl.when(jnp.logical_not(has_last))
    def _():
        wide[:, 0:HALO] = jnp.zeros((channels, HALO), jnp.float32)

    @pl.when(jnp.logical_not(has_next))
    def _():
        wide[:, samples + HALO : width] = jnp.zeros((channels, HALO), jnp.float32)

    pl.when(has_last)(to_next.wait_recv)
    pl.when(has_next)(to_last.wait_recv)

    high, low = split(wide[...])
    both = jnp.dot(
        jnp.concatenate([high, low], axis=0), fir_high, preferred_element_type=jnp.float32
    )
    filtered = (
        both[0:channels]
        + both[channels : 2 * channels]
        + jnp.dot(high, fir_low, preferred_element_type=jnp.float32)
    )
    at = time_at * samples - HALO + lax.broadcasted_iota(jnp.int32, (channels, width), 1)
    filtered = jnp.where((at >= 0) & (at < samples * time_count), filtered, 0.0)
    rows_at = lax.broadcasted_iota(jnp.int32, (width, samples), 0)
    cols_at = lax.broadcasted_iota(jnp.int32, (width, samples), 1) + HALO
    band = (jnp.abs(rows_at - cols_at) <= AVG // 2).astype(jnp.float32).astype(jnp.bfloat16)
    summed = jnp.dot(
        jnp.concatenate(split(jnp.abs(filtered)), axis=0), band, preferred_element_type=jnp.float32
    )
    local_mean = (summed[0:channels] + summed[channels : 2 * channels]) / AVG
    centre = filtered[:, HALO : HALO + samples]
    every_ref[chan_at, time_at] = (centre / (local_mean + EPSILON)).astype(jnp.bfloat16)

    sent = []

    def push(chan_from, time_from, to, wanted=None):
        block = every_ref.at[chan_from, time_from]
        copy = pltpu.make_async_remote_copy(
            src_ref=block,
            dst_ref=block,
            send_sem=send_sem.at[len(sent)],
            recv_sem=recv_sem.at[chan_from, time_from],
            device_id=to,
        )
        sent.append((wanted, copy))
        if wanted is None:
            copy.start()
        else:
            pl.when(wanted)(copy.start)

    def onward(time_from):
        even = lax.rem(jnp.abs(time_at - time_from), 2) == 0
        for hop in (2, 1):
            up = even & (time_from <= time_at) & (time_at + hop < time_count)
            push(chan_at, time_from, {"tm": time_at + hop}, up)
            down = even & (time_from >= time_at) & (time_at >= hop)
            push(chan_at, time_from, {"tm": time_at - hop}, down)

    def arrived(chan_from, time_from):
        block = every_ref.at[chan_from, time_from]
        pltpu.make_async_remote_copy(
            src_ref=block,
            dst_ref=block,
            send_sem=send_sem.at[0],
            recv_sem=recv_sem.at[chan_from, time_from],
            device_id=sibling,
        ).wait_recv()

    for step, time_from in enumerate(times):
        if step:
            arrived(chan_at, time_from)
        onward(time_from)
        for chan_to in others:
            push(chan_at, time_from, {"chan": chan_to})
        push(chan_at, time_from, sibling)
        if step:
            for chan_from in others:
                arrived(chan_from, times[step - 1])
                push(chan_from, times[step - 1], sibling)
    for chan_from in others:
        arrived(chan_from, times[-1])
        push(chan_from, times[-1], sibling)
    for time_from in times:
        for chan_from in [chan_at] + others:
            arrived(chan_from + 1 - 2 * core_at, time_from)
    for wanted, copy in sent:
        if wanted is None:
            copy.wait_send()
        else:
            pl.when(wanted)(copy.wait_send)
    pl.when(has_next)(to_next.wait_send)
    pl.when(has_last)(to_last.wait_send)


def correlate(row_share, scaling, matchings_ref, every_ref, out_ref):
    _, time_count, group_ch, samples_dev = every_ref.shape
    match_count = matchings_ref.shape[0]
    samples = time_count * samples_dev
    chan_at, time_at = lax.axis_index("chan"), lax.axis_index("tm")
    depth = samples + MAXLAG
    width = samples + 2 * MAXLAG
    rows = -(-row_share // 16) * 16
    row_at = time_at * row_share
    start = pl.multiple_of(row_at // rows * rows, rows)
    margin = jnp.zeros((rows, MAXLAG), jnp.bfloat16)
    blocks = [every_ref[chan_at, at, pl.ds(start, rows), :] for at in range(time_count)]
    own = jnp.concatenate([margin] + blocks + [margin], axis=1).astype(jnp.float32)
    if rows != row_share:
        own = pltpu.roll(own, rows - lax.rem(row_at, rows), 0)
    tail = jnp.zeros((group_ch, MAXLAG), jnp.bfloat16)
    weights = []
    for match in range(match_count):
        partner = matchings_ref[match, chan_at]
        blocks = [every_ref[partner, at] for at in range(time_count)]
        ahead = jnp.concatenate(blocks + [tail], axis=1)
        behind = pltpu.roll(ahead.astype(jnp.float32), 1, 1).astype(jnp.bfloat16)
        weights += [behind, ahead]
    weights = jnp.concatenate(weights, axis=0)
    pair = 2 * group_ch
    per_chunk = 16
    for first in range(0, LAGS, 2 * per_chunk):
        lags = range(first, min(first + 2 * per_chunk, LAGS), 2)
        lagged = jnp.concatenate(
            [
                pltpu.roll(own, (lag - (2 * MAXLAG - 1)) % width, 1)[:, :depth].astype(jnp.bfloat16)
                for lag in lags
            ],
            axis=0,
        )
        summed = lax.dot_general(
            lagged, weights, (((1,), (1,)), ((), ())), preferred_element_type=jnp.float32
        )
        scaled = (summed * scaling).astype(jnp.bfloat16)
        for at, lag in enumerate(lags):
            span = min(pair, (LAGS - lag) * group_ch)
            for match in range(match_count):
                out_ref[match, 0, :, lag * group_ch : lag * group_ch + span] = scaled[
                    at * rows : at * rows + row_share, match * pair : match * pair + span
                ]


def local(records, fir_taps, matchings):
    group_ch, samples_dev = records.shape
    group_count, time_count = lax.axis_size("chan"), lax.axis_size("tm")
    match_count = matchings.shape[0]
    width = samples_dev + 2 * HALO
    chips = group_count // CORES
    sends = time_count * (2 * chips + 3)
    every = pl.pallas_call(
        functools.partial(gather, time_count, group_count),
        out_shape=jax.ShapeDtypeStruct(
            (group_count, time_count, group_ch, samples_dev), jnp.bfloat16
        ),
        in_specs=[pl.BlockSpec(memory_space=pltpu.VMEM)] * 2,
        out_specs=pl.BlockSpec(memory_space=pltpu.VMEM),
        scratch_shapes=[
            pltpu.VMEM((group_ch, width), jnp.float32),
            pltpu.VMEM((8, width), jnp.float32),
            pltpu.SemaphoreType.DMA((2,)),
            pltpu.SemaphoreType.DMA((2,)),
            pltpu.SemaphoreType.DMA((sends,)),
            pltpu.SemaphoreType.DMA((group_count, time_count)),
        ],
        compiler_params=pltpu.CompilerParams(collective_id=0, has_side_effects=True),
    )(records, fir_taps.reshape(1, -1))
    row_share = group_ch // time_count
    scaling = 1.0 / math.sqrt(samples_dev * time_count)
    return pl.pallas_call(
        functools.partial(correlate, row_share, scaling),
        out_shape=jax.ShapeDtypeStruct(
            (match_count, 1, row_share, LAGS * group_ch), jnp.bfloat16
        ),
        in_specs=[
            pl.BlockSpec(memory_space=pltpu.SMEM),
            pl.BlockSpec(memory_space=pltpu.VMEM),
        ],
        out_specs=pl.BlockSpec(memory_space=pltpu.VMEM),
    )(matchings, every)


def solution(mesh):
    in_specs = (P(("parts", "chan"), "tm"), P(), P())
    out_specs = P(None, ("parts", "chan"), "tm", None)
    return jax.shard_map(local, mesh=mesh, in_specs=in_specs, out_specs=out_specs, check_vma=False)
```

```python
import functools
import math

import jax
import jax.numpy as jnp
from jax import lax
from jax.experimental import pallas as pl
from jax.experimental.pallas import tpu as pltpu
from jax.sharding import PartitionSpec as P

AVG = 65
MAXLAG = 128
LAGS = 257
HALO = 128
CORES = 2

EPSILON = 1e-05


def split(values):
    high = values.astype(jnp.bfloat16)
    low = (values - high.astype(jnp.float32)).astype(jnp.bfloat16)
    return high, low


def flipped(at, step, count):
    if count & (count - 1):
        return lax.rem(at + step, count)
    bit = 1
    while bit <= step:
        if step & bit:
            at = at + bit * (1 - 2 * lax.rem(at // bit, 2))
        bit *= 2
    return at


def gather(
    time_count,
    group_count,
    records_ref,
    taps_ref,
    every_ref,
    wide,
    taps_row,
    halo_send,
    halo_recv,
    send_sem,
    recv_sem,
):
    time_at, chan_at = lax.axis_index("tm"), lax.axis_index("chan")
    channels, samples = records_ref.shape
    width = samples + 2 * HALO
    chips = group_count // CORES
    chip_at, core_at = chan_at // CORES, lax.rem(chan_at, CORES)
    sibling = {"chan": chan_at + 1 - 2 * core_at}
    times = [flipped(time_at, step, time_count) for step in range(time_count)]
    others = [
        lax.rem(chip_at + step, chips) * CORES + core_at for step in range(1, chips)
    ]

    barrier = pltpu.get_barrier_semaphore()
    cross = [at + 1 - 2 * core_at for at in others]
    peers = [{"tm": at} for at in times[1:]] + [{"chan": at} for at in others + cross] + [sibling]
    for peer in peers:
        pl.semaphore_signal(barrier, inc=1, device_id=peer)

    taps_row[...] = jnp.zeros_like(taps_row)
    taps_row[0:1, 0 : taps_ref.shape[1]] = taps_ref[...]
    tap_half = taps_ref.shape[1] // 2
    fir = pltpu.roll(
        jnp.broadcast_to(taps_row[0:1, :], (width, width)),
        width - tap_half,
        1,
        stride=1,
        stride_axis=0,
    )
    fir_high, fir_low = split(fir)
    pl.semaphore_wait(barrier, len(peers))

    def halo(source, target, side, to):
        return pltpu.make_async_remote_copy(
            src_ref=records_ref.at[:, source],
            dst_ref=wide.at[:, target],
            send_sem=halo_send.at[side],
            recv_sem=halo_recv.at[side],
            device_id={"tm": to},
        )

    to_next = halo(pl.ds(samples - HALO, HALO), pl.ds(0, HALO), 0, time_at + 1)
    to_last = halo(pl.ds(0, HALO), pl.ds(samples + HALO, HALO), 1, time_at - 1)
    has_next, has_last = time_at < time_count - 1, time_at > 0
    pl.when(has_next)(to_next.start)
    pl.when(has_last)(to_last.start)
    wide[:, HALO : HALO + samples] = records_ref[...]

    @pl.when(jnp.logical_not(has_last))
    def _():
        wide[:, 0:HALO] = jnp.zeros((channels, HALO), jnp.float32)

    @pl.when(jnp.logical_not(has_next))
    def _():
        wide[:, samples + HALO : width] = jnp.zeros((channels, HALO), jnp.float32)

    pl.when(has_last)(to_next.wait_recv)
    pl.when(has_next)(to_last.wait_recv)

    high, low = split(wide[...])
    both = jnp.dot(
        jnp.concatenate([high, low], axis=0), fir_high, preferred_element_type=jnp.float32
    )
    filtered = (
        both[0:channels]
        + both[channels : 2 * channels]
        + jnp.dot(high, fir_low, preferred_element_type=jnp.float32)
    )
    at = time_at * samples - HALO + lax.broadcasted_iota(jnp.int32, (channels, width), 1)
    filtered = jnp.where((at >= 0) & (at < samples * time_count), filtered, 0.0)
    rows_at = lax.broadcasted_iota(jnp.int32, (width, samples), 0)
    cols_at = lax.broadcasted_iota(jnp.int32, (width, samples), 1) + HALO
    band = (jnp.abs(rows_at - cols_at) <= AVG // 2).astype(jnp.float32).astype(jnp.bfloat16)
    summed = jnp.dot(
        jnp.concatenate(split(jnp.abs(filtered)), axis=0), band, preferred_element_type=jnp.float32
    )
    local_mean = (summed[0:channels] + summed[channels : 2 * channels]) / AVG
    centre = filtered[:, HALO : HALO + samples]
    every_ref[chan_at, time_at] = (centre / (local_mean + EPSILON)).astype(jnp.bfloat16)

    sent = []

    def push(chan_from, time_from, to):
        block = every_ref.at[chan_from, time_from]
        copy = pltpu.make_async_remote_copy(
            src_ref=block,
            dst_ref=block,
            send_sem=send_sem.at[len(sent)],
            recv_sem=recv_sem.at[chan_from, time_from],
            device_id=to,
        )
        copy.start()
        sent.append(copy)

    def arrived(chan_from, time_from):
        block = every_ref.at[chan_from, time_from]
        pltpu.make_async_remote_copy(
            src_ref=block,
            dst_ref=block,
            send_sem=send_sem.at[0],
            recv_sem=recv_sem.at[chan_from, time_from],
            device_id=sibling,
        ).wait_recv()

    for time_to in reversed(times[1:]):
        push(chan_at, time_at, {"tm": time_to})
    for step, time_from in enumerate(times):
        if step:
            arrived(chan_at, time_from)
        for chan_to in others + cross:
            push(chan_at, time_from, {"chan": chan_to})
        push(chan_at, time_from, sibling)
    for time_from in times:
        for chan_from in others + cross:
            arrived(chan_from, time_from)
        arrived(chan_at + 1 - 2 * core_at, time_from)
    for copy in sent:
        copy.wait_send()
    pl.when(has_next)(to_next.wait_send)
    pl.when(has_last)(to_last.wait_send)


def correlate(row_share, scaling, matchings_ref, every_ref, out_ref):
    _, time_count, group_ch, samples_dev = every_ref.shape
    match_count = matchings_ref.shape[0]
    samples = time_count * samples_dev
    chan_at, time_at = lax.axis_index("chan"), lax.axis_index("tm")
    depth = samples + MAXLAG
    width = samples + 2 * MAXLAG
    rows = -(-row_share // 16) * 16
    row_at = time_at * row_share
    start = pl.multiple_of(row_at // rows * rows, rows)
    margin = jnp.zeros((rows, MAXLAG), jnp.bfloat16)
    blocks = [every_ref[chan_at, at, pl.ds(start, rows), :] for at in range(time_count)]
    own = jnp.concatenate([margin] + blocks + [margin], axis=1).astype(jnp.float32)
    if rows != row_share:
        own = pltpu.roll(own, rows - lax.rem(row_at, rows), 0)
    tail = jnp.zeros((group_ch, MAXLAG), jnp.bfloat16)
    weights = []
    for match in range(match_count):
        partner = matchings_ref[match, chan_at]
        blocks = [every_ref[partner, at] for at in range(time_count)]
        ahead = jnp.concatenate(blocks + [tail], axis=1)
        behind = pltpu.roll(ahead.astype(jnp.float32), 1, 1).astype(jnp.bfloat16)
        weights += [behind, ahead]
    weights = jnp.concatenate(weights, axis=0)
    pair = 2 * group_ch
    per_chunk = 16
    for first in range(0, LAGS, 2 * per_chunk):
        lags = range(first, min(first + 2 * per_chunk, LAGS), 2)
        lagged = jnp.concatenate(
            [
                pltpu.roll(own, (lag - (2 * MAXLAG - 1)) % width, 1)[:, :depth].astype(jnp.bfloat16)
                for lag in lags
            ],
            axis=0,
        )
        summed = lax.dot_general(
            lagged, weights, (((1,), (1,)), ((), ())), preferred_element_type=jnp.float32
        )
        scaled = (summed * scaling).astype(jnp.bfloat16)
        for at, lag in enumerate(lags):
            span = min(pair, (LAGS - lag) * group_ch)
            for match in range(match_count):
                out_ref[match, 0, :, lag * group_ch : lag * group_ch + span] = scaled[
                    at * rows : at * rows + row_share, match * pair : match * pair + span
                ]


def local(records, fir_taps, matchings):
    group_ch, samples_dev = records.shape
    group_count, time_count = lax.axis_size("chan"), lax.axis_size("tm")
    match_count = matchings.shape[0]
    width = samples_dev + 2 * HALO
    chips = group_count // CORES
    sends = time_count - 1 + time_count * (4 * chips)
    every = pl.pallas_call(
        functools.partial(gather, time_count, group_count),
        out_shape=jax.ShapeDtypeStruct(
            (group_count, time_count, group_ch, samples_dev), jnp.bfloat16
        ),
        in_specs=[pl.BlockSpec(memory_space=pltpu.VMEM)] * 2,
        out_specs=pl.BlockSpec(memory_space=pltpu.VMEM),
        scratch_shapes=[
            pltpu.VMEM((group_ch, width), jnp.float32),
            pltpu.VMEM((8, width), jnp.float32),
            pltpu.SemaphoreType.DMA((2,)),
            pltpu.SemaphoreType.DMA((2,)),
            pltpu.SemaphoreType.DMA((sends,)),
            pltpu.SemaphoreType.DMA((group_count, time_count)),
        ],
        compiler_params=pltpu.CompilerParams(collective_id=0, has_side_effects=True),
    )(records, fir_taps.reshape(1, -1))
    row_share = group_ch // time_count
    scaling = 1.0 / math.sqrt(samples_dev * time_count)
    return pl.pallas_call(
        functools.partial(correlate, row_share, scaling),
        out_shape=jax.ShapeDtypeStruct(
            (match_count, 1, row_share, LAGS * group_ch), jnp.bfloat16
        ),
        in_specs=[
            pl.BlockSpec(memory_space=pltpu.SMEM),
            pl.BlockSpec(memory_space=pltpu.VMEM),
        ],
        out_specs=pl.BlockSpec(memory_space=pltpu.VMEM),
    )(matchings, every)


def solution(mesh):
    in_specs = (P(("parts", "chan"), "tm"), P(), P())
    out_specs = P(None, ("parts", "chan"), "tm", None)
    return jax.shard_map(local, mesh=mesh, in_specs=in_specs, out_specs=out_specs, check_vma=False)
```

```python
import functools
import math

import jax
import jax.numpy as jnp
from jax import lax
from jax.experimental import pallas as pl
from jax.experimental.pallas import tpu as pltpu
from jax.sharding import PartitionSpec as P

AVG = 65
MAXLAG = 128
LAGS = 257
HALO = 128
CORES = 2

EPSILON = 1e-05


def split(values):
    high = values.astype(jnp.bfloat16)
    low = (values - high.astype(jnp.float32)).astype(jnp.bfloat16)
    return high, low


def flipped(at, step, count):
    if count & (count - 1):
        return lax.rem(at + step, count)
    bit = 1
    while bit <= step:
        if step & bit:
            at = at + bit * (1 - 2 * lax.rem(at // bit, 2))
        bit *= 2
    return at


def gather(
    time_count,
    group_count,
    records_ref,
    every_ref,
    send_sem,
    recv_sem,
):
    time_at, chan_at = lax.axis_index("tm"), lax.axis_index("chan")
    chips = group_count // CORES
    chip_at, core_at = chan_at // CORES, lax.rem(chan_at, CORES)
    sibling = {"chan": chan_at + 1 - 2 * core_at}
    times = [flipped(time_at, step, time_count) for step in range(time_count)]
    others = [
        lax.rem(chip_at + step, chips) * CORES + core_at for step in range(1, chips)
    ]

    barrier = pltpu.get_barrier_semaphore()
    cross = [at + 1 - 2 * core_at for at in others]
    peers = [{"tm": at} for at in times[1:]] + [{"chan": at} for at in others + cross] + [sibling]
    for peer in peers:
        pl.semaphore_signal(barrier, inc=1, device_id=peer)

    every_ref[chan_at, time_at] = records_ref[...].astype(jnp.bfloat16)
    pl.semaphore_wait(barrier, len(peers))

    sent = []

    def push(chan_from, time_from, to):
        block = every_ref.at[chan_from, time_from]
        copy = pltpu.make_async_remote_copy(
            src_ref=block,
            dst_ref=block,
            send_sem=send_sem.at[len(sent)],
            recv_sem=recv_sem.at[chan_from, time_from],
            device_id=to,
        )
        copy.start()
        sent.append(copy)

    def arrived(chan_from, time_from):
        block = every_ref.at[chan_from, time_from]
        pltpu.make_async_remote_copy(
            src_ref=block,
            dst_ref=block,
            send_sem=send_sem.at[0],
            recv_sem=recv_sem.at[chan_from, time_from],
            device_id=sibling,
        ).wait_recv()

    for time_to in reversed(times[1:]):
        push(chan_at, time_at, {"tm": time_to})
    for step, time_from in enumerate(times):
        if step:
            arrived(chan_at, time_from)
        for chan_to in others + cross:
            push(chan_at, time_from, {"chan": chan_to})
        push(chan_at, time_from, sibling)
    for time_from in times:
        for chan_from in others + cross:
            arrived(chan_from, time_from)
        arrived(chan_at + 1 - 2 * core_at, time_from)
    for copy in sent:
        copy.wait_send()


def normalize(values, taps_ref, taps_row, block):
    rows, samples = values.shape
    width = block + 2 * HALO
    starts = range(0, samples, block)
    taps_row[...] = jnp.zeros_like(taps_row)
    taps_row[0:1, 0 : taps_ref.shape[1]] = taps_ref[...]
    fir = pltpu.roll(
        jnp.broadcast_to(taps_row[0:1, :], (width, width)),
        width - taps_ref.shape[1] // 2,
        1,
        stride=1,
        stride_axis=0,
    )[:, HALO : HALO + block]
    rows_at = lax.broadcasted_iota(jnp.int32, (width, block), 0)
    cols_at = lax.broadcasted_iota(jnp.int32, (width, block), 1) + HALO
    band = (jnp.abs(rows_at - cols_at) <= AVG // 2).astype(jnp.float32).astype(jnp.bfloat16)

    def spans(values):
        margin = jnp.zeros((rows, HALO), values.dtype)
        padded = jnp.concatenate([margin, values, margin], axis=1)
        return jnp.concatenate([padded[:, at : at + width] for at in starts], axis=0)

    def dot(left, right):
        return jnp.dot(left, right, preferred_element_type=jnp.float32)

    fir_high, fir_low = split(fir)
    wide = spans(values)
    filtered = dot(wide, fir_high) + dot(wide, fir_low)
    merged = jnp.concatenate(
        [filtered[at : at + rows] for at in range(0, rows * len(starts), rows)], axis=1
    )
    high, low = split(jnp.abs(merged))
    summed = dot(spans(high), band) + dot(spans(low), band)
    normed = (filtered / (summed / AVG + EPSILON)).astype(jnp.bfloat16)
    return jnp.concatenate(
        [normed[at : at + rows] for at in range(0, rows * len(starts), rows)], axis=1
    )


def correlate(row_share, scaling, matchings_ref, taps_ref, every_ref, out_ref, taps_row):
    _, time_count, group_ch, samples_dev = every_ref.shape
    match_count = matchings_ref.shape[0]
    samples = time_count * samples_dev
    chan_at, time_at = lax.axis_index("chan"), lax.axis_index("tm")
    depth = samples + MAXLAG
    width = samples + 2 * MAXLAG
    rows = -(-row_share // 16) * 16
    row_at = time_at * row_share
    start = pl.multiple_of(row_at // rows * rows, rows)
    picked = [[every_ref[chan_at, at, pl.ds(start, rows), :] for at in range(time_count)]]
    for match in range(match_count):
        partner = matchings_ref[match, chan_at]
        picked.append([every_ref[partner, at] for at in range(time_count)])
    picked = jnp.concatenate([jnp.concatenate(blocks, axis=1) for blocks in picked], axis=0)
    normed = normalize(picked, taps_ref, taps_row, samples_dev)
    margin = jnp.zeros((rows, MAXLAG), jnp.bfloat16)
    own = jnp.concatenate([margin, normed[0:rows], margin], axis=1).astype(jnp.float32)
    if rows != row_share:
        own = pltpu.roll(own, rows - lax.rem(row_at, rows), 0)
    tail = jnp.zeros((group_ch, MAXLAG), jnp.bfloat16)
    weights = []
    for match in range(match_count):
        at = rows + match * group_ch
        ahead = jnp.concatenate([normed[at : at + group_ch], tail], axis=1)
        behind = pltpu.roll(ahead.astype(jnp.float32), 1, 1).astype(jnp.bfloat16)
        weights += [behind, ahead]
    weights = jnp.concatenate(weights, axis=0)
    pair = 2 * group_ch
    per_chunk = 16
    for first in range(0, LAGS, 2 * per_chunk):
        lags = range(first, min(first + 2 * per_chunk, LAGS), 2)
        lagged = jnp.concatenate(
            [
                pltpu.roll(own, (lag - (2 * MAXLAG - 1)) % width, 1)[:, :depth].astype(jnp.bfloat16)
                for lag in lags
            ],
            axis=0,
        )
        summed = lax.dot_general(
            lagged, weights, (((1,), (1,)), ((), ())), preferred_element_type=jnp.float32
        )
        scaled = (summed * scaling).astype(jnp.bfloat16)
        for at, lag in enumerate(lags):
            span = min(pair, (LAGS - lag) * group_ch)
            for match in range(match_count):
                out_ref[match, 0, :, lag * group_ch : lag * group_ch + span] = scaled[
                    at * rows : at * rows + row_share, match * pair : match * pair + span
                ]


def local(records, fir_taps, matchings):
    group_ch, samples_dev = records.shape
    group_count, time_count = lax.axis_size("chan"), lax.axis_size("tm")
    match_count = matchings.shape[0]
    chips = group_count // CORES
    sends = time_count - 1 + time_count * (4 * chips)
    every = pl.pallas_call(
        functools.partial(gather, time_count, group_count),
        out_shape=jax.ShapeDtypeStruct(
            (group_count, time_count, group_ch, samples_dev), jnp.bfloat16
        ),
        in_specs=[pl.BlockSpec(memory_space=pltpu.VMEM)],
        out_specs=pl.BlockSpec(memory_space=pltpu.VMEM),
        scratch_shapes=[
            pltpu.SemaphoreType.DMA((sends,)),
            pltpu.SemaphoreType.DMA((group_count, time_count)),
        ],
        compiler_params=pltpu.CompilerParams(collective_id=0, has_side_effects=True),
    )(records)
    row_share = group_ch // time_count
    scaling = 1.0 / math.sqrt(samples_dev * time_count)
    return pl.pallas_call(
        functools.partial(correlate, row_share, scaling),
        out_shape=jax.ShapeDtypeStruct(
            (match_count, 1, row_share, LAGS * group_ch), jnp.bfloat16
        ),
        in_specs=[
            pl.BlockSpec(memory_space=pltpu.SMEM),
            pl.BlockSpec(memory_space=pltpu.VMEM),
            pl.BlockSpec(memory_space=pltpu.VMEM),
        ],
        out_specs=pl.BlockSpec(memory_space=pltpu.VMEM),
        scratch_shapes=[pltpu.VMEM((8, samples_dev + 2 * HALO), jnp.float32)],
    )(matchings, fir_taps.reshape(1, -1), every)


def solution(mesh):
    in_specs = (P(("parts", "chan"), "tm"), P(), P())
    out_specs = P(None, ("parts", "chan"), "tm", None)
    return jax.shard_map(local, mesh=mesh, in_specs=in_specs, out_specs=out_specs, check_vma=False)
```

```python
import functools
import math

import jax
import jax.numpy as jnp
from jax import lax
from jax.experimental import pallas as pl
from jax.experimental.pallas import tpu as pltpu
from jax.sharding import PartitionSpec as P

AVG = 65
MAXLAG = 128
LAGS = 257
HALO = 128
CORES = 2

EPSILON = 1e-05


def split(values):
    high = values.astype(jnp.bfloat16)
    low = (values - high.astype(jnp.float32)).astype(jnp.bfloat16)
    return high, low


def flipped(at, step, count):
    if count & (count - 1):
        return lax.rem(at + step, count)
    bit = 1
    while bit <= step:
        if step & bit:
            at = at + bit * (1 - 2 * lax.rem(at // bit, 2))
        bit *= 2
    return at


def prepare(taps_ref, taps_row, block):
    width = block + 2 * HALO
    taps_row[...] = jnp.zeros_like(taps_row)
    taps_row[0:1, 0 : taps_ref.shape[1]] = taps_ref[...]
    fir = pltpu.roll(
        jnp.broadcast_to(taps_row[0:1, :], (width, width)),
        width - taps_ref.shape[1] // 2,
        1,
        stride=1,
        stride_axis=0,
    )[:, HALO : HALO + block]
    rows_at = lax.broadcasted_iota(jnp.int32, (width, block), 0)
    cols_at = lax.broadcasted_iota(jnp.int32, (width, block), 1) + HALO
    band = (jnp.abs(rows_at - cols_at) <= AVG // 2).astype(jnp.float32).astype(jnp.bfloat16)
    return split(fir) + (band,)


def normalize(values, prepared, block):
    fir_high, fir_low, band = prepared
    rows, samples = values.shape
    width = block + 2 * HALO
    starts = range(0, samples, block)

    def spans(values):
        margin = jnp.zeros((rows, HALO), values.dtype)
        padded = jnp.concatenate([margin, values, margin], axis=1)
        return jnp.concatenate([padded[:, at : at + width] for at in starts], axis=0)

    def dot(left, right):
        return jnp.dot(left, right, preferred_element_type=jnp.float32)

    wide = spans(values)
    filtered = dot(wide, fir_high) + dot(wide, fir_low)
    merged = jnp.concatenate(
        [filtered[at : at + rows] for at in range(0, rows * len(starts), rows)], axis=1
    )
    high, low = split(jnp.abs(merged))
    summed = dot(spans(high), band) + dot(spans(low), band)
    normed = (filtered / (summed / AVG + EPSILON)).astype(jnp.bfloat16)
    return jnp.concatenate(
        [normed[at : at + rows] for at in range(0, rows * len(starts), rows)], axis=1
    )


def gather(
    time_count,
    group_count,
    row_share,
    scaling,
    matchings_hbm,
    taps_hbm,
    records_hbm,
    out_ref,
    matchings_ref,
    taps_ref,
    records_ref,
    load_sem,
    every_ref,
    lagged_ref,
    taps_row,
    send_sem,
    recv_sem,
):
    time_at, chan_at = lax.axis_index("tm"), lax.axis_index("chan")
    chips = group_count // CORES
    chip_at, core_at = chan_at // CORES, lax.rem(chan_at, CORES)
    sibling = {"chan": chan_at + 1 - 2 * core_at}
    times = [flipped(time_at, step, time_count) for step in range(time_count)]
    others = [
        lax.rem(chip_at + step, chips) * CORES + core_at for step in range(1, chips)
    ]

    barrier = pltpu.get_barrier_semaphore()
    cross = [at + 1 - 2 * core_at for at in others]
    peers = [{"tm": at} for at in times[1:]] + [{"chan": at} for at in others + cross] + [sibling]
    for peer in peers:
        pl.semaphore_signal(barrier, inc=1, device_id=peer)

    loads = [
        pltpu.make_async_copy(source, target, load_sem.at[at])
        for at, (source, target) in enumerate(
            (
                (records_hbm, records_ref),
                (taps_hbm, taps_ref),
                (matchings_hbm, matchings_ref),
            )
        )
    ]
    for load in loads:
        load.start()
    for load in loads:
        load.wait()
    every_ref[chan_at, time_at] = records_ref[...].astype(jnp.bfloat16)
    pl.semaphore_wait(barrier, len(peers))

    sent = []

    def push(chan_from, time_from, to):
        block = every_ref.at[chan_from, time_from]
        copy = pltpu.make_async_remote_copy(
            src_ref=block,
            dst_ref=block,
            send_sem=send_sem.at[len(sent)],
            recv_sem=recv_sem.at[chan_from, time_from],
            device_id=to,
        )
        copy.start()
        sent.append(copy)

    def arrived(chan_from, time_from):
        block = every_ref.at[chan_from, time_from]
        pltpu.make_async_remote_copy(
            src_ref=block,
            dst_ref=block,
            send_sem=send_sem.at[0],
            recv_sem=recv_sem.at[chan_from, time_from],
            device_id=sibling,
        ).wait_recv()

    for time_to in reversed(times[1:]):
        push(chan_at, time_at, {"tm": time_to})
    for step, time_from in enumerate(times):
        if step:
            arrived(chan_at, time_from)
        for chan_to in others + cross:
            push(chan_at, time_from, {"chan": chan_to})
        push(chan_at, time_from, sibling)
    samples_dev = every_ref.shape[3]
    group_ch, match_count = every_ref.shape[2], matchings_ref.shape[0]
    samples = time_count * samples_dev
    depth, width = samples + MAXLAG, samples + 2 * MAXLAG
    rows = -(-row_share // 16) * 16
    row_at = time_at * row_share
    start = pl.multiple_of(row_at // rows * rows, rows)
    prepared = prepare(taps_ref, taps_row, samples_dev)
    own = jnp.concatenate(
        [every_ref[chan_at, at, pl.ds(start, rows), :] for at in range(time_count)], axis=1
    )
    own = normalize(own, prepared, samples_dev)
    margin = jnp.zeros((rows, MAXLAG), jnp.bfloat16)
    own = jnp.concatenate([margin, own, margin], axis=1).astype(jnp.float32)
    if rows != row_share:
        own = pltpu.roll(own, rows - lax.rem(row_at, rows), 0)
    for lag in range(0, LAGS, 2):
        shifted = pltpu.roll(own, (lag - (2 * MAXLAG - 1)) % width, 1)[:, :depth]
        lagged_ref[lag // 2 * rows : (lag // 2 + 1) * rows, :] = shifted.astype(jnp.bfloat16)
    for time_from in times:
        for chan_from in others + cross:
            arrived(chan_from, time_from)
        arrived(chan_at + 1 - 2 * core_at, time_from)
    picked = []
    for match in range(match_count):
        partner = matchings_ref[match, chan_at]
        picked.append(
            jnp.concatenate([every_ref[partner, at] for at in range(time_count)], axis=1)
        )
    normed = normalize(jnp.concatenate(picked, axis=0), prepared, samples_dev)
    tail = jnp.zeros((group_ch, MAXLAG), jnp.bfloat16)
    weights = []
    for match in range(match_count):
        at = match * group_ch
        ahead = jnp.concatenate([normed[at : at + group_ch], tail], axis=1)
        behind = pltpu.roll(ahead.astype(jnp.float32), 1, 1).astype(jnp.bfloat16)
        weights += [behind, ahead]
    weights = jnp.concatenate(weights, axis=0)
    pair = 2 * group_ch
    per_chunk = 16
    for first in range(0, LAGS, 2 * per_chunk):
        lags = range(first, min(first + 2 * per_chunk, LAGS), 2)
        lagged = lagged_ref[first // 2 * rows : (first // 2 + len(lags)) * rows, :]
        summed = lax.dot_general(
            lagged, weights, (((1,), (1,)), ((), ())), preferred_element_type=jnp.float32
        )
        scaled = (summed * scaling).astype(jnp.bfloat16)
        for at, lag in enumerate(lags):
            span = min(pair, (LAGS - lag) * group_ch)
            for match in range(match_count):
                out_ref[match, 0, :, lag * group_ch : lag * group_ch + span] = scaled[
                    at * rows : at * rows + row_share, match * pair : match * pair + span
                ]
    for copy in sent:
        copy.wait_send()


def local(records, fir_taps, matchings):
    group_ch, samples_dev = records.shape
    group_count, time_count = lax.axis_size("chan"), lax.axis_size("tm")
    match_count = matchings.shape[0]
    chips = group_count // CORES
    sends = time_count - 1 + time_count * (4 * chips)
    samples = samples_dev * time_count
    row_share = group_ch // time_count
    rows = -(-row_share // 16) * 16
    scaling = 1.0 / math.sqrt(samples)
    return pl.pallas_call(
        functools.partial(gather, time_count, group_count, row_share, scaling),
        out_shape=jax.ShapeDtypeStruct(
            (match_count, 1, row_share, LAGS * group_ch), jnp.bfloat16
        ),
        in_specs=[pl.BlockSpec(memory_space=pltpu.HBM)] * 3,
        out_specs=pl.BlockSpec(memory_space=pltpu.VMEM),
        scratch_shapes=[
            pltpu.SMEM(matchings.shape, jnp.int32),
            pltpu.VMEM((1,) + fir_taps.shape, jnp.float32),
            pltpu.VMEM(records.shape, jnp.float32),
            pltpu.SemaphoreType.DMA((3,)),
            pltpu.VMEM((group_count, time_count, group_ch, samples_dev), jnp.bfloat16),
            pltpu.VMEM(((LAGS + 1) // 2 * rows, samples + MAXLAG), jnp.bfloat16),
            pltpu.VMEM((8, samples_dev + 2 * HALO), jnp.float32),
            pltpu.SemaphoreType.DMA((sends,)),
            pltpu.SemaphoreType.DMA((group_count, time_count)),
        ],
        compiler_params=pltpu.CompilerParams(vmem_limit_bytes=40<<20, collective_id=0, has_side_effects=True),
    )(matchings, fir_taps.reshape(1, -1), records)


def solution(mesh):
    in_specs = (P(("parts", "chan"), "tm"), P(), P())
    out_specs = P(None, ("parts", "chan"), "tm", None)
    return jax.shard_map(local, mesh=mesh, in_specs=in_specs, out_specs=out_specs, check_vma=False)
```

```python
import functools
import math

import jax
import jax.numpy as jnp
from jax import lax
from jax.experimental import pallas as pl
from jax.experimental.pallas import tpu as pltpu
from jax.sharding import PartitionSpec as P

AVG = 65
MAXLAG = 128
LAGS = 257
HALO = 128
CORES = 2

EPSILON = 1e-05


def split(values):
    high = values.astype(jnp.bfloat16)
    low = (values - high.astype(jnp.float32)).astype(jnp.bfloat16)
    return high, low


def flipped(at, step, count):
    if count & (count - 1):
        return lax.rem(at + step, count)
    bit = 1
    while bit <= step:
        if step & bit:
            at = at + bit * (1 - 2 * lax.rem(at // bit, 2))
        bit *= 2
    return at


def prepare(taps_ref, taps_row, block):
    width = block + 2 * HALO
    taps_row[...] = jnp.zeros_like(taps_row)
    taps_row[0:1, 0 : taps_ref.shape[1]] = taps_ref[...]
    fir = pltpu.roll(
        jnp.broadcast_to(taps_row[0:1, :], (width, width)),
        width - taps_ref.shape[1] // 2,
        1,
        stride=1,
        stride_axis=0,
    )[:, HALO : HALO + block]
    rows_at = lax.broadcasted_iota(jnp.int32, (width, block), 0)
    cols_at = lax.broadcasted_iota(jnp.int32, (width, block), 1) + HALO
    band = (jnp.abs(rows_at - cols_at) <= AVG // 2).astype(jnp.float32).astype(jnp.bfloat16)
    return split(fir) + (band,)


def normalize(values, prepared, block):
    fir_high, fir_low, band = prepared
    rows, samples = values.shape
    width = block + 2 * HALO
    starts = range(0, samples, block)

    def spans(values):
        margin = jnp.zeros((rows, HALO), values.dtype)
        padded = jnp.concatenate([margin, values, margin], axis=1)
        return jnp.concatenate([padded[:, at : at + width] for at in starts], axis=0)

    def dot(left, right):
        return jnp.dot(left, right, preferred_element_type=jnp.float32)

    wide = spans(values)
    filtered = dot(wide, fir_high) + dot(wide, fir_low)
    merged = jnp.concatenate(
        [filtered[at : at + rows] for at in range(0, rows * len(starts), rows)], axis=1
    )
    high, low = split(jnp.abs(merged))
    summed = dot(spans(high), band) + dot(spans(low), band)
    normed = (filtered / (summed / AVG + EPSILON)).astype(jnp.bfloat16)
    return jnp.concatenate(
        [normed[at : at + rows] for at in range(0, rows * len(starts), rows)], axis=1
    )


def gather(
    time_count,
    group_count,
    row_share,
    scaling,
    matchings_hbm,
    taps_hbm,
    records_hbm,
    out_ref,
    matchings_ref,
    taps_ref,
    records_ref,
    load_sem,
    every_ref,
    lagged_ref,
    taps_row,
    send_sem,
    recv_sem,
):
    time_at, chan_at = lax.axis_index("tm"), lax.axis_index("chan")
    chips = group_count // CORES
    chip_at, core_at = chan_at // CORES, lax.rem(chan_at, CORES)
    sibling = {"chan": chan_at + 1 - 2 * core_at}
    times = [flipped(time_at, step, time_count) for step in range(time_count)]
    others = [
        lax.rem(chip_at + step, chips) * CORES + core_at for step in range(1, chips)
    ]

    barrier = pltpu.get_barrier_semaphore()
    cross = [at + 1 - 2 * core_at for at in others]
    peers = [{"tm": at} for at in times[1:]] + [{"chan": at} for at in others + cross] + [sibling]
    for peer in peers:
        pl.semaphore_signal(barrier, inc=1, device_id=peer)

    loads = [
        pltpu.make_async_copy(source, target, load_sem.at[at])
        for at, (source, target) in enumerate(
            (
                (records_hbm, records_ref),
                (taps_hbm, taps_ref),
                (matchings_hbm, matchings_ref),
            )
        )
    ]
    for load in loads:
        load.start()
    for load in loads:
        load.wait()
    every_ref[chan_at, time_at] = records_ref[...].astype(jnp.bfloat16)
    samples_dev = every_ref.shape[3]
    prepared = prepare(taps_ref, taps_row, samples_dev)
    pl.semaphore_wait(barrier, len(peers))

    sent = []

    def push(chan_from, time_from, to):
        block = every_ref.at[chan_from, time_from]
        copy = pltpu.make_async_remote_copy(
            src_ref=block,
            dst_ref=block,
            send_sem=send_sem.at[len(sent)],
            recv_sem=recv_sem.at[chan_from, time_from],
            device_id=to,
        )
        copy.start()
        sent.append(copy)

    def arrived(chan_from, time_from):
        block = every_ref.at[chan_from, time_from]
        pltpu.make_async_remote_copy(
            src_ref=block,
            dst_ref=block,
            send_sem=send_sem.at[0],
            recv_sem=recv_sem.at[chan_from, time_from],
            device_id=sibling,
        ).wait_recv()

    for time_to in reversed(times[1:]):
        push(chan_at, time_at, {"tm": time_to})
    for step, time_from in enumerate(times):
        if step:
            arrived(chan_at, time_from)
        for chan_to in others + cross:
            push(chan_at, time_from, {"chan": chan_to})
        push(chan_at, time_from, sibling)
    group_ch, match_count = every_ref.shape[2], matchings_ref.shape[0]
    samples = time_count * samples_dev
    depth, width = samples + MAXLAG, samples + 2 * MAXLAG
    rows = -(-row_share // 16) * 16
    row_at = time_at * row_share
    start = pl.multiple_of(row_at // rows * rows, rows)
    own = jnp.concatenate(
        [every_ref[chan_at, at, pl.ds(start, rows), :] for at in range(time_count)], axis=1
    )
    own = normalize(own, prepared, samples_dev)
    margin = jnp.zeros((rows, MAXLAG), jnp.bfloat16)
    own = jnp.concatenate([margin, own, margin], axis=1).astype(jnp.float32)
    if rows != row_share:
        own = pltpu.roll(own, rows - lax.rem(row_at, rows), 0)
    for lag in range(0, LAGS, 2):
        shifted = pltpu.roll(own, (lag - (2 * MAXLAG - 1)) % width, 1)[:, :depth]
        lagged_ref[lag // 2 * rows : (lag // 2 + 1) * rows, :] = shifted.astype(jnp.bfloat16)
    for time_from in times:
        for chan_from in others + cross:
            arrived(chan_from, time_from)
        arrived(chan_at + 1 - 2 * core_at, time_from)
    picked = []
    for match in range(match_count):
        partner = matchings_ref[match, chan_at]
        picked.append(
            jnp.concatenate([every_ref[partner, at] for at in range(time_count)], axis=1)
        )
    normed = normalize(jnp.concatenate(picked, axis=0), prepared, samples_dev)
    tail = jnp.zeros((group_ch, MAXLAG), jnp.bfloat16)
    weights = []
    for match in range(match_count):
        at = match * group_ch
        ahead = jnp.concatenate([normed[at : at + group_ch], tail], axis=1)
        behind = pltpu.roll(ahead.astype(jnp.float32), 1, 1).astype(jnp.bfloat16)
        weights += [behind, ahead]
    weights = jnp.concatenate(weights, axis=0)
    pair = 2 * group_ch
    per_chunk = 16
    for first in range(0, LAGS, 2 * per_chunk):
        lags = range(first, min(first + 2 * per_chunk, LAGS), 2)
        lagged = lagged_ref[first // 2 * rows : (first // 2 + len(lags)) * rows, :]
        summed = lax.dot_general(
            lagged, weights, (((1,), (1,)), ((), ())), preferred_element_type=jnp.float32
        )
        scaled = (summed * scaling).astype(jnp.bfloat16)
        for at, lag in enumerate(lags):
            span = min(pair, (LAGS - lag) * group_ch)
            for match in range(match_count):
                out_ref[match, 0, :, lag * group_ch : lag * group_ch + span] = scaled[
                    at * rows : at * rows + row_share, match * pair : match * pair + span
                ]
    for copy in sent:
        copy.wait_send()


def local(records, fir_taps, matchings):
    group_ch, samples_dev = records.shape
    group_count, time_count = lax.axis_size("chan"), lax.axis_size("tm")
    match_count = matchings.shape[0]
    chips = group_count // CORES
    sends = time_count - 1 + time_count * (4 * chips)
    samples = samples_dev * time_count
    row_share = group_ch // time_count
    rows = -(-row_share // 16) * 16
    scaling = 1.0 / math.sqrt(samples)
    return pl.pallas_call(
        functools.partial(gather, time_count, group_count, row_share, scaling),
        out_shape=jax.ShapeDtypeStruct(
            (match_count, 1, row_share, LAGS * group_ch), jnp.bfloat16
        ),
        in_specs=[pl.BlockSpec(memory_space=pltpu.HBM)] * 3,
        out_specs=pl.BlockSpec(memory_space=pltpu.VMEM),
        scratch_shapes=[
            pltpu.SMEM(matchings.shape, jnp.int32),
            pltpu.VMEM((1,) + fir_taps.shape, jnp.float32),
            pltpu.VMEM(records.shape, jnp.float32),
            pltpu.SemaphoreType.DMA((3,)),
            pltpu.VMEM((group_count, time_count, group_ch, samples_dev), jnp.bfloat16),
            pltpu.VMEM(((LAGS + 1) // 2 * rows, samples + MAXLAG), jnp.bfloat16),
            pltpu.VMEM((8, samples_dev + 2 * HALO), jnp.float32),
            pltpu.SemaphoreType.DMA((sends,)),
            pltpu.SemaphoreType.DMA((group_count, time_count)),
        ],
        compiler_params=pltpu.CompilerParams(collective_id=0, has_side_effects=True),
    )(matchings, fir_taps.reshape(1, -1), records)


def solution(mesh):
    in_specs = (P(("parts", "chan"), "tm"), P(), P())
    out_specs = P(None, ("parts", "chan"), "tm", None)
    return jax.shard_map(local, mesh=mesh, in_specs=in_specs, out_specs=out_specs, check_vma=False)
```
